256 devices in a mesh: dp: 16 (over y, z_hi), mp: 16 (over x, z_lo, core).
Axes of the slice: x: 4, y: 4, z: 8 (z_hi: 4, z_lo: 2; z = z_hi * 2 + z_lo), core: 2. Of those that a mesh axis runs over, the one named last changes fastest.
Arguments:
- inputs: bfloat16 [16, 512, 4096], P('dp', None, 'mp'), may hold values from -6 to 6
- out_grads: bfloat16 [16, 512, 4096], P('dp', None, 'mp'), may hold values from -6 to 6
- gate_weight: bfloat16 [4096, 14336], P('dp', 'mp'), may hold values from -0.09375 to 0.09375
- down_weight: bfloat16 [14336, 4096], P('mp', 'dp'), may hold values from -0.046875 to 0.046875
- in_proj: bfloat16 [4096, 64], replicated, may hold values from -0.09375 to 0.09375
- out_proj: bfloat16 [14336, 64], P('mp'), may hold values from -0.046875 to 0.046875
- in_precond: float32 [64, 64], replicated, may hold values from -0.75 to 0.75
- out_precond: float32 [64, 64], replicated, may hold values from -0.75 to 0.75
- queries: bfloat16 [2048, 4096], P('dp', 'mp'), may hold values from -48 to 48
- languages: int32 [2048], P('dp'), may hold values from 0 to 31, as said below
Outputs:
- influence: float32 [16, 32], P('dp')
The draws below stay inside these ranges and needn't reach their ends.
Inputs may be any that keep to these rules, and one draw needn't show every extreme that they name: Each of the 32 languages labels exactly 64 queries.
All inputs are finite; a program needn't handle non-finite values.
Results may differ from the reference program's by a relative error of at most 0.0042.
Values may be sent and summed in bfloat16 or wider, within the bound.
No kernel may reach another device: no remote copies, remote signals or barrier semaphores. Data moves between devices by JAX's collectives and lax.ppermute only.
A program may use at most 128 MiB of HBM per device.

```python
import jax
import jax.numpy as jnp
from jax import lax

D = 4096
FF = 14336
R = 64
SEQ = 512
LANGS = 32
EXAMPLES = 16
QUERIES = 2048


def draw_languages(key, part):
    order = jax.random.permutation(key, QUERIES)
    return (order % LANGS).astype(jnp.int32)


def shard_levels(rng, extent, cuts, smallest, high):
    def one(axis_at, parts):
        heights = jax.random.uniform(jax.random.fold_in(jax.random.fold_in(rng, 6), axis_at), (parts,), jnp.float32, smallest / len(cuts), high / len(cuts))
        return jnp.repeat(jnp.exp(heights), extent[axis_at] // parts).reshape((-1,) + (1,) * (len(extent) - axis_at - 1))

    loudness = one(*cuts[0])
    for cut in cuts[1:]:
        loudness = loudness * one(*cut)
    return loudness


def normal_values(stream_key, shape, scale, limit, pieces=(), held_as=jnp.bfloat16):
    level = shard_levels(stream_key, shape, pieces, -0.22, 0.18) if pieces else 1.0
    result = jax.random.normal(stream_key, shape, jnp.float32) * scale * level
    return jnp.minimum(jnp.maximum(result, -limit), limit).astype(held_as)


def setup_inputs(seed: int = 0) -> dict:
    key_of = jax.random.split(jax.random.key(seed), 11)
    return {
        "inputs": normal_values(key_of[0], (EXAMPLES, SEQ, D), 1.0, 6.0, ((0, 16), (2, 16))),
        "out_grads": normal_values(key_of[1], (EXAMPLES, SEQ, D), 1.0, 6.0, ((0, 16), (2, 16))),
        "gate_weight": normal_values(key_of[2], (D, FF), D ** -0.5, 0.09375, ((0, 16), (1, 16))),
        "down_weight": normal_values(key_of[3], (FF, D), FF ** -0.5, 0.046875, ((0, 16), (1, 16))),
        "in_proj": normal_values(key_of[4], (D, R), D ** -0.5, 0.09375),
        "out_proj": normal_values(key_of[5], (FF, R), FF ** -0.5, 0.046875, ((0, 16),)),
        "in_precond": normal_values(key_of[6], (R, R), R ** -0.5, 0.75, (), jnp.float32),
        "out_precond": normal_values(key_of[7], (R, R), R ** -0.5, 0.75, (), jnp.float32),
        "queries": normal_values(key_of[8], (QUERIES, R * R), 8.0, 48.0, ((0, 16), (1, 16))),
        "languages": draw_languages(jax.random.fold_in(key_of[10], 71), 0),
    }


def reference(inputs, out_grads, gate_weight, down_weight, in_proj, out_proj, in_precond, out_precond, queries, languages):
    def one_example(pair):
        rows, grads = pair
        gate = jnp.dot(rows, gate_weight, preferred_element_type=jnp.float32)
        hidden_grad = jnp.dot(grads, down_weight.T, preferred_element_type=jnp.float32)
        up_grad = (hidden_grad * jax.nn.silu(gate)).astype(jnp.bfloat16)
        in_factor = jnp.dot(jnp.dot(rows, in_proj, preferred_element_type=jnp.float32), in_precond.T, precision=lax.Precision.HIGHEST)
        out_factor = jnp.dot(jnp.dot(up_grad, out_proj, preferred_element_type=jnp.float32), out_precond, precision=lax.Precision.HIGHEST)
        full = jnp.dot(in_factor.T, out_factor, precision=lax.Precision.HIGHEST) / SEQ
        return full.reshape(R * R).astype(jnp.bfloat16)

    projected = lax.map(one_example, (inputs, out_grads))
    scores = jnp.dot(projected, queries.T, preferred_element_type=jnp.float32)
    onehot = (languages[:, None] == jnp.arange(LANGS, dtype=jnp.int32)[None, :]).astype(jnp.float32)
    summed = jnp.dot(scores, onehot, precision=lax.Precision.HIGHEST)
    return summed / (QUERIES // LANGS)
```

```python
import jax
import jax.numpy as jnp
from jax import lax
from jax.experimental import pallas as pl
from jax.experimental.pallas import tpu as pltpu
from jax.sharding import PartitionSpec as P

LANGS = 32
AXES = ("dp", "mp")
HIGH = lax.Precision.HIGHEST
F32 = jnp.float32


def flat(x, y, z, c):
    x, y, z = x % 4, y % 4, z % 8
    return (y * 4 + (z >> 1)) * 16 + x * 4 + (z & 1) * 2 + c


def perm_of(move):
    pairs = []
    for d in range(16):
        for m in range(16):
            place = (m >> 2, d >> 2, ((d & 3) << 1) | ((m >> 1) & 1), m & 1)
            there = move(*place)
            if there is not None:
                pairs.append((flat(*place), flat(*there)))
    return pairs


def send(v, move):
    return lax.ppermute(v, AXES, perm_of(move))


def ring(v, axis, ready=()):
    plus = (lambda x, y, z, c: (x + 1, y, z, c)) if axis == "x" else (lambda x, y, z, c: (x, y + 1, z, c))
    minus = (lambda x, y, z, c: (x - 1, y, z, c)) if axis == "x" else (lambda x, y, z, c: (x, y - 1, z, c))
    v, *ready = lax.optimization_barrier((v, *ready))
    half = v.shape[0] // 2
    before = send(v, plus)
    after = send(v, minus)
    low = send(before[:half], plus)
    high = send(after[half:], minus)
    return [v, before, after, low, high], ready


def weight_a(x, y, z, c):
    return (x, y, z + 4, c) if c == (z >> 1) & 1 else (x, y, z + 2, 1 - c)


def weight_b(x, y, z, c):
    return (x, y, z, c) if c == (z >> 1) & 1 else (x, y, z - 2, 1 - c)


def coords():
    d, m = lax.axis_index("dp"), lax.axis_index("mp")
    y, zhh, zhl = d // 4, (d // 2) % 2, d % 2
    x, zl, c = m // 4, (m // 2) % 2, m % 2
    return x, y, zhh, zhl, zl, c


def source_bit(zhh, zhl, c):
    same = (c + zhl + 1) % 2
    stays = (1 - same) * zhl
    return (zhh + 1 - stays) % 2


def matmul_kernel(gate, *refs):
    own, near, far, ws = refs[:5], refs[5:10], refs[10:15], refs[15:20]
    refs = refs[20:]
    if gate:
        _, proj, out, pout, xv, wv, xsem, wsem = refs
    else:
        out, xv, wv, xsem, wsem = refs
    x, y, zhh, zhl, zl, c = coords()
    bit = source_bit(zhh, zhl, c)
    base = 0 if gate else 512
    copies = []
    for s in range(4):
        row = ((s // 2 + c) % 2) * 512
        low = (zl + s % 2) % 2
        for n, step in enumerate((0, 3, 1, 2)):
            col = (((x + step) % 4) * 2 + low) * 256
            dst = xv.at[pl.ds(pl.multiple_of(row, 512), 512), pl.ds(pl.multiple_of(col, 256), 256)]
            if s < 2:
                group = (own, near)[s]
                src = group[3 + (0 if gate else 1)] if step == 2 else group[n].at[pl.ds(base, 512), :]
            elif step == 2:
                src = far[3 + s - 2].at[0, pl.ds(base, 512), :]
            else:
                src = far[n].at[s - 2, pl.ds(base, 512), :]
            copies.append(pltpu.make_async_copy(src, dst, xsem.at[s * 4 + n]))
    for r in range(2):
        h = bit if r == 0 else 1 - bit
        for n, step in enumerate((0, 3, 1, 2)):
            at = pl.ds(pl.multiple_of((((y + step) % 4) * 2 + h) * 256, 256), 256)
            dst = wv.at[at, :] if gate else wv.at[:, at]
            src = ws[3 + r].at[0] if step == 2 else ws[n].at[r]
            copies.append(pltpu.make_async_copy(src, dst, wsem.at[r * 4 + n]))
    for copy in copies:
        copy.start()
    for copy in copies:
        copy.wait()

    @pl.loop(0, 4)
    def _(i):
        at = pl.ds(pl.multiple_of(i * 256, 256), 256)
        rows = xv[at, :]
        if gate:
            out[at, :] = jnp.dot(rows, wv[...], preferred_element_type=F32)
            pout[at, :] = jnp.dot(rows, proj[...], preferred_element_type=F32)
        else:
            out[at, :] = lax.dot_general(rows, wv[...], (((1,), (1,)), ((), ())), preferred_element_type=F32)


def matmul(gate, blocks, *more):
    hbm = pl.BlockSpec(memory_space=pl.ANY)
    vmem = pl.BlockSpec(memory_space=pltpu.VMEM)
    shapes = [jax.ShapeDtypeStruct((1024, 896), F32)]
    if gate:
        shapes += [jax.ShapeDtypeStruct((1024, 64), F32)]
    wshape = (2048, 896) if gate else (896, 2048)
    return pl.pallas_call(
        lambda *refs: matmul_kernel(gate, *refs),
        out_shape=shapes,
        in_specs=[hbm] * 20 + ([hbm, vmem] if gate else []),
        out_specs=[vmem] * len(shapes),
        scratch_shapes=[
            pltpu.VMEM((1024, 2048), jnp.bfloat16),
            pltpu.VMEM(wshape, jnp.bfloat16),
            pltpu.SemaphoreType.DMA((16,)),
            pltpu.SemaphoreType.DMA((8,)),
        ],
        compiler_params=pltpu.CompilerParams(vmem_limit_bytes=48 << 20),
        cost_estimate=pl.CostEstimate(flops=2 * 1024 * 2048 * 960, bytes_accessed=12 << 20, transcendentals=0),
    )(*blocks, *more)


def everyone(v, axis):
    return lax.all_to_all(jnp.broadcast_to(v[None], (16,) + v.shape), axis, 0, 0, tiled=True)


def shards(inputs, out_grads, gate_weight, down_weight, in_proj, out_proj, in_precond, out_precond, queries, languages):
    x, y, zhh, zhl, zl, c = coords()
    swap = lambda x, y, z, c: (x, y, z, 1 - c)

    with jax.named_scope("language_sums"):
        onehot = (languages[None, :] == jnp.arange(LANGS, dtype=jnp.int32)[:, None]).astype(jnp.bfloat16)
        mine = jnp.dot(onehot, queries, preferred_element_type=F32)
        feature_block = jnp.sum(everyone(mine, "dp").reshape(16, LANGS, 256), axis=0)
        by_language = everyone(feature_block, "mp").reshape(16, LANGS, 256)

    with jax.named_scope("along_z"):
        both = jnp.concatenate([inputs[0], out_grads[0]], axis=0)
        turn = lambda v, k: send(v, lambda x, y, z, c: (x, y, z ^ k, c))
        ga = send(gate_weight, weight_a)
        gb = send(gate_weight, weight_b)
        both1, ga = lax.optimization_barrier((both, ga))
        near = turn(both1, 1)
        both2, gb = lax.optimization_barrier((both, gb))
        far2 = turn(both2, 2)
        both3, near = lax.optimization_barrier((both, near))
        far3 = turn(both3, 3)
        down2, far2 = lax.optimization_barrier((down_weight, far2))
        da = send(down2, weight_a)
        down3, far3 = lax.optimization_barrier((down_weight, far3))
        db = send(down3, weight_b)
    with jax.named_scope("along_x"):
        own_ring, _ = ring(both, "x")
        near_ring, own_ring[1:3] = ring(near, "x", own_ring[1:3])
        far_ring, near_ring[1:3] = ring(jnp.stack([far2, far3]), "x", near_ring[1:3])
    with jax.named_scope("along_y"):
        gate_ring, _ = ring(jnp.stack([ga, gb]), "y")
        down_ring, gate_ring[1:3] = ring(jnp.stack([da, db]), "y", gate_ring[1:3])
    tokens = own_ring + near_ring + far_ring

    proj_half = lax.dynamic_index_in_dim(in_proj.reshape(8, 2, 256, 64), c, 1, keepdims=False).reshape(2048, 64)
    out_mine = jnp.where(c == zhl, out_proj, send(out_proj, swap))

    gate, in_sum = matmul(True, tokens + gate_ring, by_language, proj_half)
    gate = gate[:512] + send(gate[512:], swap)
    in_sum = in_sum[:512] + send(in_sum[512:], swap)
    (hidden_grad,) = matmul(False, tokens + down_ring)
    hidden_grad = hidden_grad[:512] + send(hidden_grad[512:], swap)

    with jax.named_scope("finish"):
        up_grad = (hidden_grad * jax.nn.silu(gate)).astype(jnp.bfloat16)
        out_part = jnp.dot(up_grad, out_mine, preferred_element_type=F32)
        outer = lax.dot_general(in_sum, out_part, (((0,), (0,)), ((), ())), precision=HIGH)
        outer = send(outer, lambda x, y, z, c: (x, y, z ^ 2, c) if c else (x, y, z, c))
        total = jnp.sum(everyone(outer, "mp").reshape(16, 64, 64), axis=0)
        full = jnp.dot(jnp.dot(in_precond, total, precision=HIGH), out_precond, precision=HIGH) / 512
        projected = full.astype(jnp.bfloat16).astype(F32)
        by_language = by_language.transpose(1, 0, 2).reshape(LANGS, 64, 64)
        scores = jnp.sum(projected[None] * by_language, axis=(1, 2))
    return (scores / 64).reshape(1, LANGS)


def solution(mesh):
    return jax.shard_map(
        shards,
        mesh=mesh,
        in_specs=(
            P("dp", None, "mp"),
            P("dp", None, "mp"),
            P("dp", "mp"),
            P("mp", "dp"),
            P(),
            P("mp", None),
            P(),
            P(),
            P("dp", "mp"),
            P("dp"),
        ),
        out_specs=P("dp", None),
        check_vma=False,
    )
```

```python
import jax
import jax.numpy as jnp
from jax import lax
from jax.experimental import pallas as pl
from jax.experimental.pallas import tpu as pltpu
from jax.sharding import PartitionSpec as P

LANGS = 32
AXES = ("dp", "mp")
HIGH = lax.Precision.HIGHEST
F32 = jnp.float32


def flat(x, y, z, c):
    x, y, z = x % 4, y % 4, z % 8
    return (y * 4 + (z >> 1)) * 16 + x * 4 + (z & 1) * 2 + c


def perm_of(move):
    pairs = []
    for d in range(16):
        for m in range(16):
            place = (m >> 2, d >> 2, ((d & 3) << 1) | ((m >> 1) & 1), m & 1)
            there = move(*place)
            if there is not None:
                pairs.append((flat(*place), flat(*there)))
    return pairs


def send(v, move):
    return lax.ppermute(v, AXES, perm_of(move))


def first(v, *ready):
    return lax.optimization_barrier((v, *ready))


def ring_moves(axis):
    if axis == "x":
        return (lambda x, y, z, c: (x + 1, y, z, c)), (lambda x, y, z, c: (x - 1, y, z, c))
    return (lambda x, y, z, c: (x, y + 1, z, c)), (lambda x, y, z, c: (x, y - 1, z, c))


def ring_near(v, axis):
    plus, minus = ring_moves(axis)
    return send(v, plus), send(v, minus)


def ring_far(before, after, axis):
    plus, minus = ring_moves(axis)
    half = before.shape[0] // 2
    return send(before[:half], plus), send(after[half:], minus)


def weight_a(x, y, z, c):
    return (x, y, z + 4, c) if c == (z >> 1) & 1 else (x, y, z + 2, 1 - c)


def weight_b(x, y, z, c):
    return (x, y, z, c) if c == (z >> 1) & 1 else (x, y, z - 2, 1 - c)


def coords():
    d, m = lax.axis_index("dp"), lax.axis_index("mp")
    y, zhh, zhl = d // 4, (d // 2) % 2, d % 2
    x, zl, c = m // 4, (m // 2) % 2, m % 2
    return x, y, zhh, zhl, zl, c


def source_bit(zhh, zhl, c):
    same = (c + zhl + 1) % 2
    stays = (1 - same) * zhl
    return (zhh + 1 - stays) % 2


def token_copies(which, late, refs, xv, sem, x, zhh, zhl, zl, c):
    copies = []
    for s in range(2):
        low = (zl + s + (zl + zhl) % 2) % 2 if late else (zl + s) % 2
        for n, step in enumerate((0, 3, 1, 2)):
            col = pl.multiple_of((((x + step) % 4) * 2 + low) * 256, 256)
            for t in range(2):
                row = pl.multiple_of(((t + c) % 2) * 256, 256)
                if step == 2:
                    src = refs[s * 5 + 3 + which].at[pl.ds(t * 256, 256), :]
                else:
                    src = refs[s * 5 + n].at[pl.ds(which * 512 + t * 256, 256), :]
                dst = xv.at[pl.ds(row, 256), pl.ds(col, 256)]
                copies.append(pltpu.make_async_copy(src, dst, sem.at[(s * 4 + n) * 2 + t]))
    return copies


def gate_copies(ref, proj, wv, sem, bit, c):
    copies = []
    for n in range(8):
        src = proj.at[pl.ds(pl.multiple_of((n * 2 + c) * 256, 256), 256), :]
        copies.append(pltpu.make_async_copy(src, wv.at[pl.ds(n * 256, 256), pl.ds(896, 128)], sem.at[8 + n]))
    for r in range(2):
        h = bit if r == 0 else 1 - bit
        for n in range(4):
            row = pl.multiple_of((n * 2 + h) * 256, 256)
            copies.append(pltpu.make_async_copy(ref.at[n, r], wv.at[pl.ds(row, 256), pl.ds(0, 896)], sem.at[r * 4 + n]))
    return copies


def down_copies(ref, wv, sem, bit):
    copies = []
    for r in range(2):
        h = bit if r == 0 else 1 - bit
        for n in range(4):
            col = pl.multiple_of((n * 2 + h) * 256, 256)
            src = ref.at[n, r, pl.ds(0, 896), :]
            copies.append(pltpu.make_async_copy(src, wv.at[:, pl.ds(col, 256)], sem.at[r * 4 + n]))
    return copies


def matmul_kernel(gate, hidden, late, *refs):
    refs = list(refs)
    take = lambda n: [refs.pop(0) for _ in range(n)]
    blocks = take(10)
    gw, proj = take(2) if gate else (None, None)
    dw = take(1)[0] if hidden else None
    take(1)
    gouts = take(2) if gate else []
    houts = take(2) if hidden else []
    gscr = take(4) if gate else []
    hscr = take(4) if hidden else []
    x, y, zhh, zhl, zl, c = coords()
    bit = source_bit(zhh, zhl, c)
    gcopies = hcopies = []
    if gate:
        gcopies = gate_copies(gw, proj, gscr[1], gscr[3], bit, c)
        gcopies = gcopies + token_copies(0, late, blocks, gscr[0], gscr[2], x, zhh, zhl, zl, c)
    if hidden:
        hcopies = down_copies(dw, hscr[1], hscr[3], bit)
        hcopies = hcopies + token_copies(1, late, blocks, hscr[0], hscr[2], x, zhh, zhl, zl, c)
    for copy in gcopies + hcopies:
        copy.start()

    def products(copies, scr, outs, contract):
        for copy in copies:
            copy.wait()

        @pl.loop(0, 2)
        def _(i):
            rows = scr[0][pl.ds(pl.multiple_of(i * 256, 256), 256), :]
            product = lax.dot_general(rows, scr[1][...], (((1,), (contract,)), ((), ())), preferred_element_type=F32)
            for part in range(2):
                @pl.when(i == part)
                def _():
                    outs[part][...] = product

    if gate:
        products(gcopies, gscr, gouts, 0)
    if hidden:
        products(hcopies, hscr, houts, 1)


def matmul(late, blocks, after, gate=None, proj=None, down=None):
    hbm = pl.BlockSpec(memory_space=pltpu.MemorySpace.HBM)
    vmem = pl.BlockSpec(memory_space=pltpu.VMEM)
    shapes, scratch = [], []
    args = list(blocks)
    for there, wshape in ((gate is not None, (2048, 1024)), (down is not None, (896, 2048))):
        if there:
            width = wshape[1] if wshape[0] == 2048 else 896
            shapes += [jax.ShapeDtypeStruct((256, width), F32)] * 2
            scratch += [
                pltpu.VMEM((512, 2048), jnp.bfloat16),
                pltpu.VMEM(wshape, jnp.bfloat16),
                pltpu.SemaphoreType.DMA((16,)),
                pltpu.SemaphoreType.DMA((16,)),
            ]
    if gate is not None:
        args += [gate, proj]
    if down is not None:
        args += [down]
    args += [after]
    flops = 2 * 512 * 2048 * 960 * ((gate is not None) + (down is not None))
    return pl.pallas_call(
        lambda *refs: matmul_kernel(gate is not None, down is not None, late, *refs),
        out_shape=shapes,
        in_specs=[hbm] * len(args),
        out_specs=[vmem] * len(shapes),
        scratch_shapes=scratch,
        compiler_params=pltpu.CompilerParams(vmem_limit_bytes=60 << 20),
        cost_estimate=pl.CostEstimate(flops=flops, bytes_accessed=10 << 20, transcendentals=0),
    )(*args)


def everyone(v, axis):
    return lax.all_to_all(jnp.broadcast_to(v[None], (16,) + v.shape), axis, 0, 0, tiled=True)


def shards(inputs, out_grads, gate_weight, down_weight, in_proj, out_proj, in_precond, out_precond, queries, languages):
    x, y, zhh, zhl, zl, c = coords()
    swap = lambda x, y, z, c: (x, y, z, 1 - c)
    rings = [[y * 4 + h for y in range(4)] for h in range(4)]

    hold = lax.optimization_barrier
    in_proj = jnp.pad(in_proj, ((0, 0), (0, 64)))
    with jax.named_scope("language_sums"):
        onehot = (languages[None, :] == jnp.arange(LANGS, dtype=jnp.int32)[:, None]).astype(jnp.bfloat16)
        mine = jnp.dot(onehot, queries, preferred_element_type=F32)
        high = lax.reduce_precision(mine, 8, 7)
        halves = [high.astype(jnp.bfloat16), (mine - high).astype(jnp.bfloat16)]
        down_weight = jnp.concatenate([down_weight, *halves], axis=0)
    inward = lambda x, y, z, c: (x, y, z ^ 3, c) if z % 4 in (1, 2) else None
    outward = lambda x, y, z, c: (x, y, z ^ 1, c) if z % 4 in (1, 2) else None
    with jax.named_scope("first_moves"):
        ga = send(gate_weight, weight_a)
        gb = send(gate_weight, weight_b)
        both = jnp.concatenate([inputs[0], out_grads[0]], axis=0)
        near = send(both, lambda x, y, z, c: (x, y, z ^ 1, c))
        inner_a = send(both, inward)
        own1, own2 = ring_near(both, "x")
        gates = lax.all_gather(jnp.stack([ga, gb]), "dp", axis_index_groups=rings)
        out_mine = jnp.where(c == zhl, out_proj, send(out_proj, swap))
        near, inner_a, own1, own2, down_weight, out_mine, in_proj, ga = hold(
            (near, inner_a, own1, own2, down_weight, out_mine, in_proj, ga)
        )
    with jax.named_scope("second_moves"):
        da = send(down_weight, weight_a)
        db = send(down_weight, weight_b)
        inner_b = send(near, inward)
        outer_a = send(inner_a, outward)
        near1, near2 = ring_near(near, "x")
        inner_b, outer_a, da, db, near1, near2 = hold((inner_b, outer_a, da, db, near1, near2))
    with jax.named_scope("third_moves"):
        downs = lax.all_gather(jnp.stack([da, db]), "dp", axis_index_groups=rings)
        far_a = jnp.where(zl == zhl, outer_a, inner_a)
        outer_b = send(inner_b, outward)
        fa1, fa2 = ring_near(far_a, "x")
        near3, near4 = ring_far(near1, near2, "x")
        outer_b, fa1, fa2, near3, near4, own1, own2 = hold((outer_b, fa1, fa2, near3, near4, own1, own2))
    with jax.named_scope("fourth_moves"):
        far_b = jnp.where(zl == zhl, outer_b, inner_b)
        fb1, fb2 = ring_near(far_b, "x")
        fa3, fa4 = ring_far(fa1, fa2, "x")
        own3, own4 = ring_far(own1, own2, "x")
        fb1, fb2, fa3, fa4, own3, own4 = hold((fb1, fb2, fa3, fa4, own3, own4))
    early = [both, own1, own2, own3, own4, near, near1, near2, near3, near4]
    with jax.named_scope("fifth_moves"):
        fb3, fb4 = ring_far(fb1, fb2, "x")
        gate0 = matmul(False, early, fb1, gate=gates, proj=in_proj)
        hidden0 = matmul(False, early, gate0[1], down=downs)
    late = [far_a, fa1, fa2, fa3, fa4, far_b, fb1, fb2, fb3, fb4]

    def finish(gate, gate_other, hidden, hidden_other):
        gate = gate + send(gate_other, swap)
        hidden_grad = hidden + send(hidden_other, swap)
        up_grad = (hidden_grad * jax.nn.silu(gate[:, :896])).astype(jnp.bfloat16)
        out_part = jnp.dot(up_grad, out_mine, preferred_element_type=F32)
        return lax.dot_general(gate[:, 896:960], out_part, (((0,), (0,)), ((), ())), precision=HIGH)

    with jax.named_scope("second_half"):
        both1 = matmul(True, late, hidden0[1], gate=gates, proj=in_proj, down=downs)
        outer1 = finish(*both1)
    with jax.named_scope("first_half"):
        outer0 = finish(*gate0, *hidden0)

    with jax.named_scope("language_sums"):
        sums = jnp.sum(downs[:, :, 896:].astype(F32).reshape(16, LANGS, 256), axis=0)
        sums = sums + send(sums, swap)
        by_language = jnp.where(c == zhl, sums, send(sums, lambda x, y, z, c: (x, y, z ^ 2, c)))

    with jax.named_scope("finish"):
        outers = outer0 + send(outer1, lambda x, y, z, c: (x, y, z ^ 2, c))
        part = jnp.dot(jnp.dot(in_precond, outers, precision=HIGH), out_precond, precision=HIGH) / 512
        bands = lax.all_to_all(part.reshape(16, 256), "mp", 0, 0, tiled=True)
        projected = lax.reduce_precision(jnp.sum(bands, axis=0), 8, 7)
        scores = jnp.sum(projected[None, :] * by_language, axis=1)
        scores = jnp.sum(everyone(scores, "mp").reshape(16, LANGS), axis=0)
    return (scores / 64).reshape(1, LANGS)


def solution(mesh):
    return jax.shard_map(
        shards,
        mesh=mesh,
        in_specs=(
            P("dp", None, "mp"),
            P("dp", None, "mp"),
            P("dp", "mp"),
            P("mp", "dp"),
            P(),
            P("mp", None),
            P(),
            P(),
            P("dp", "mp"),
            P("dp"),
        ),
        out_specs=P("dp", None),
        check_vma=False,
    )
```

```python
import jax
import jax.numpy as jnp
from jax import lax
from jax.experimental import pallas as pl
from jax.experimental.pallas import tpu as pltpu
from jax.sharding import PartitionSpec as P

LANGS = 32
AXES = ("dp", "mp")
HIGH = lax.Precision.HIGHEST
F32 = jnp.float32


def flat(x, y, z, c):
    x, y, z = x % 4, y % 4, z % 8
    return (y * 4 + (z >> 1)) * 16 + x * 4 + (z & 1) * 2 + c


def perm_of(move):
    pairs = []
    for d in range(16):
        for m in range(16):
            place = (m >> 2, d >> 2, ((d & 3) << 1) | ((m >> 1) & 1), m & 1)
            there = move(*place)
            if there is not None:
                pairs.append((flat(*place), flat(*there)))
    return pairs


def send(v, move):
    return lax.ppermute(v, AXES, perm_of(move))


def first(v, *ready):
    return lax.optimization_barrier((v, *ready))


def ring_moves(axis):
    if axis == "x":
        return (lambda x, y, z, c: (x + 1, y, z, c)), (lambda x, y, z, c: (x - 1, y, z, c))
    return (lambda x, y, z, c: (x, y + 1, z, c)), (lambda x, y, z, c: (x, y - 1, z, c))


def ring_near(v, axis):
    plus, minus = ring_moves(axis)
    return send(v, plus), send(v, minus)


def ring_far(before, after, axis):
    plus, minus = ring_moves(axis)
    half = before.shape[0] // 2
    return send(before[:half], plus), send(after[half:], minus)


def weight_a(x, y, z, c):
    return (x, y, z + 4, c) if c == (z >> 1) & 1 else (x, y, z + 2, 1 - c)


def weight_b(x, y, z, c):
    return (x, y, z, c) if c == (z >> 1) & 1 else (x, y, z - 2, 1 - c)


def coords():
    d, m = lax.axis_index("dp"), lax.axis_index("mp")
    y, zhh, zhl = d // 4, (d // 2) % 2, d % 2
    x, zl, c = m // 4, (m // 2) % 2, m % 2
    return x, y, zhh, zhl, zl, c


def source_bit(zhh, zhl, c):
    same = (c + zhl + 1) % 2
    stays = (1 - same) * zhl
    return (zhh + 1 - stays) % 2


def token_copies(which, late, refs, xv, sem, x, zhh, zhl, zl, c):
    copies = []
    for s in range(2):
        low = (zl + s + (zl + zhl) % 2) % 2 if late else (zl + s) % 2
        for n, step in enumerate((0, 3, 1, 2)):
            col = pl.multiple_of((((x + step) % 4) * 2 + low) * 256, 256)
            for t in range(2):
                row = pl.multiple_of(((t + c) % 2) * 256, 256)
                if step == 2:
                    src = refs[s * 5 + 3 + which].at[pl.ds(t * 256, 256), :]
                else:
                    src = refs[s * 5 + n].at[pl.ds(which * 512 + t * 256, 256), :]
                dst = xv.at[pl.ds(row, 256), pl.ds(col, 256)]
                copies.append(pltpu.make_async_copy(src, dst, sem.at[(s * 4 + n) * 2 + t]))
    return copies


def gate_copies(ref, proj, wv, sem, bit, c):
    copies = []
    for n in range(8):
        src = proj.at[pl.ds(pl.multiple_of((n * 2 + c) * 256, 256), 256), :]
        copies.append(pltpu.make_async_copy(src, wv.at[pl.ds(n * 256, 256), pl.ds(896, 128)], sem.at[8 + n]))
    for r in range(2):
        h = bit if r == 0 else 1 - bit
        for n in range(4):
            row = pl.multiple_of((n * 2 + h) * 256, 256)
            copies.append(pltpu.make_async_copy(ref.at[n, r], wv.at[pl.ds(row, 256), pl.ds(0, 896)], sem.at[r * 4 + n]))
    return copies


def down_copies(ref, wv, sem, bit):
    copies = []
    for r in range(2):
        h = bit if r == 0 else 1 - bit
        for n in range(4):
            col = pl.multiple_of((n * 2 + h) * 256, 256)
            src = ref.at[n, r, pl.ds(0, 896), :]
            copies.append(pltpu.make_async_copy(src, wv.at[:, pl.ds(col, 256)], sem.at[r * 4 + n]))
    return copies


def gate_kernel(late, *refs):
    blocks, (weights, proj, _, keep, other, xv, wv, xsem, wsem) = refs[:10], refs[10:]
    x, y, zhh, zhl, zl, c = coords()
    copies = gate_copies(weights, proj, wv, wsem, source_bit(zhh, zhl, c), c)
    copies = copies + token_copies(0, late, blocks, xv, xsem, x, zhh, zhl, zl, c)
    for copy in copies:
        copy.start()
    for copy in copies:
        copy.wait()

    @pl.loop(0, 2)
    def _(i):
        rows = xv[pl.ds(pl.multiple_of(i * 256, 256), 256), :]
        product = jnp.dot(rows, wv[...], preferred_element_type=F32)
        for part, target in enumerate((keep, other)):
            @pl.when(i == part)
            def _():
                target[...] = product


def hidden_kernel(*refs):
    early, late, (weights, _, keep, other, xv, wv, xsem0, xsem1, wsem) = refs[:10], refs[10:20], refs[20:]
    x, y, zhh, zhl, zl, c = coords()
    first = down_copies(weights, wv, wsem, source_bit(zhh, zhl, c))
    first = first + token_copies(1, False, early, xv.at[pl.ds(0, 512), :], xsem0, x, zhh, zhl, zl, c)
    second = token_copies(1, True, late, xv.at[pl.ds(512, 512), :], xsem1, x, zhh, zhl, zl, c)
    for copy in first + second:
        copy.start()

    @pl.loop(0, 4)
    def _(i):
        for at, copies in ((0, first), (2, second)):
            @pl.when(i == at)
            def _():
                for copy in copies:
                    copy.wait()

        rows = xv[pl.ds(pl.multiple_of(i * 256, 256), 256), :]
        product = lax.dot_general(rows, wv[...], (((1,), (1,)), ((), ())), preferred_element_type=F32)
        place = pl.ds(pl.multiple_of((i // 2) * 256, 256), 256)
        for part, target in enumerate((keep, other)):
            @pl.when(i % 2 == part)
            def _():
                target[place, :] = product


def call(kernel, args, shape, scratch, flops):
    return pl.pallas_call(
        kernel,
        out_shape=[jax.ShapeDtypeStruct(shape, F32)] * 2,
        in_specs=[pl.BlockSpec(memory_space=pltpu.MemorySpace.HBM)] * len(args),
        out_specs=[pl.BlockSpec(memory_space=pltpu.VMEM)] * 2,
        scratch_shapes=scratch,
        compiler_params=pltpu.CompilerParams(vmem_limit_bytes=60 << 20),
        cost_estimate=pl.CostEstimate(flops=flops, bytes_accessed=8 << 20, transcendentals=0),
    )(*args)


def gate_matmul(late, blocks, weights, proj, after):
    scratch = [
        pltpu.VMEM((512, 2048), jnp.bfloat16),
        pltpu.VMEM((2048, 1024), jnp.bfloat16),
        pltpu.SemaphoreType.DMA((16,)),
        pltpu.SemaphoreType.DMA((16,)),
    ]
    kernel = lambda *refs: gate_kernel(late, *refs)
    return call(kernel, [*blocks, weights, proj, after], (256, 1024), scratch, 2 * 512 * 2048 * 1024)


def hidden_matmul(early, late, weights, after):
    scratch = [
        pltpu.VMEM((1024, 2048), jnp.bfloat16),
        pltpu.VMEM((896, 2048), jnp.bfloat16),
        pltpu.SemaphoreType.DMA((16,)),
        pltpu.SemaphoreType.DMA((16,)),
        pltpu.SemaphoreType.DMA((8,)),
    ]
    return call(hidden_kernel, [*early, *late, weights, after], (512, 896), scratch, 2 * 1024 * 2048 * 896)


def everyone(v, axis):
    return lax.all_to_all(jnp.broadcast_to(v[None], (16,) + v.shape), axis, 0, 0, tiled=True)


def shards(inputs, out_grads, gate_weight, down_weight, in_proj, out_proj, in_precond, out_precond, queries, languages):
    x, y, zhh, zhl, zl, c = coords()
    swap = lambda x, y, z, c: (x, y, z, 1 - c)
    rings = [[y * 4 + h for y in range(4)] for h in range(4)]

    hold = lax.optimization_barrier
    in_proj = jnp.pad(in_proj, ((0, 0), (0, 64)))
    with jax.named_scope("language_sums"):
        onehot = (languages[None, :] == jnp.arange(LANGS, dtype=jnp.int32)[:, None]).astype(jnp.bfloat16)
        mine = jnp.dot(onehot, queries, preferred_element_type=F32)
        high = lax.reduce_precision(mine, 8, 7)
        halves = [high.astype(jnp.bfloat16), (mine - high).astype(jnp.bfloat16)]
        down_weight = jnp.concatenate([down_weight, *halves], axis=0)
    inward = lambda x, y, z, c: (x, y, z ^ 3, c) if z % 4 in (1, 2) else None
    outward = lambda x, y, z, c: (x, y, z ^ 1, c) if z % 4 in (1, 2) else None
    with jax.named_scope("first_moves"):
        ga = send(gate_weight, weight_a)
        gb = send(gate_weight, weight_b)
        both = jnp.concatenate([inputs[0], out_grads[0]], axis=0)
        near = send(both, lambda x, y, z, c: (x, y, z ^ 1, c))
        inner_a = send(both, inward)
        own1, own2 = ring_near(both, "x")
        gates = lax.all_gather(jnp.stack([ga, gb]), "dp", axis_index_groups=rings)
        out_mine = jnp.where(c == zhl, out_proj, send(out_proj, swap))
        near, inner_a, own1, own2, down_weight, out_mine, in_proj, ga = hold(
            (near, inner_a, own1, own2, down_weight, out_mine, in_proj, ga)
        )
    with jax.named_scope("second_moves"):
        da = send(down_weight, weight_a)
        db = send(down_weight, weight_b)
        inner_b = send(near, inward)
        outer_a = send(inner_a, outward)
        near1, near2 = ring_near(near, "x")
        inner_b, outer_a, da, db, near1, near2 = hold((inner_b, outer_a, da, db, near1, near2))
    with jax.named_scope("third_moves"):
        downs = lax.all_gather(jnp.stack([da, db]), "dp", axis_index_groups=rings)
        far_a = jnp.where(zl == zhl, outer_a, inner_a)
        outer_b = send(inner_b, outward)
        fa1, fa2 = ring_near(far_a, "x")
        near3, near4 = ring_far(near1, near2, "x")
        own3, own4 = ring_far(own1, own2, "x")
        outer_b, fa1, fa2, near3, near4, own3, own4 = hold((outer_b, fa1, fa2, near3, near4, own3, own4))
    early = [both, own1, own2, own3, own4, near, near1, near2, near3, near4]
    with jax.named_scope("fourth_moves"):
        far_b = jnp.where(zl == zhl, outer_b, inner_b)
        fb1, fb2 = ring_near(far_b, "x")
        fa3, fa4 = ring_far(fa1, fa2, "x")
        gate0 = gate_matmul(False, early, gates, in_proj, fa1)
        fb1, fb2, fa3, fa4, *gate0 = hold((fb1, fb2, fa3, fa4, *gate0))
    with jax.named_scope("fifth_moves"):
        fb3, fb4 = ring_far(fb1, fb2, "x")
        late = [far_a, fa1, fa2, fa3, fa4, far_b, fb1, fb2, fb3, fb4]
        gate1 = gate_matmul(True, late, gates, in_proj, gate0[1])
        downs, other = hold((downs, gate1[1]))
        gate1 = [gate1[0], other]
        gate_both = [keep + send(other, swap) for keep, other in (gate0, gate1)]
    with jax.named_scope("hidden"):
        sums = jnp.sum(downs[:, :, 896:].astype(F32).reshape(16, LANGS, 256), axis=0)
        hidden, other = hidden_matmul(early, late, downs, sums)
        hidden = hidden + send(other, swap)
        sums = sums + send(sums, swap)

    def finish(gate, hidden_grad):
        up_grad = (hidden_grad * jax.nn.silu(gate[:, :896])).astype(jnp.bfloat16)
        out_part = jnp.dot(up_grad, out_mine, preferred_element_type=F32)
        return lax.dot_general(gate[:, 896:960], out_part, (((0,), (0,)), ((), ())), precision=HIGH)

    with jax.named_scope("second_half"):
        outer1 = finish(gate_both[1], hidden[256:])
    with jax.named_scope("first_half"):
        outer0 = finish(gate_both[0], hidden[:256])

    with jax.named_scope("finish"):
        moved = jnp.concatenate([jnp.pad(outer1, ((0, 0), (0, 192))), sums], axis=0)
        moved = send(moved, lambda x, y, z, c: (x, y, z ^ 2, c))
        outers = outer0 + moved[:64, :64]
        by_language = jnp.where(c == zhl, sums, moved[64:])
        part = jnp.dot(jnp.dot(in_precond, outers, precision=HIGH), out_precond, precision=HIGH) / 512
        bands = lax.all_to_all(part.reshape(16, 256), "mp", 0, 0, tiled=True)
        projected = lax.reduce_precision(jnp.sum(bands, axis=0), 8, 7)
        scores = jnp.sum(projected[None, :] * by_language, axis=1)
        scores = jnp.sum(everyone(scores, "mp").reshape(16, LANGS), axis=0)
    return (scores / 64).reshape(1, LANGS)


def solution(mesh):
    return jax.shard_map(
        shards,
        mesh=mesh,
        in_specs=(
            P("dp", None, "mp"),
            P("dp", None, "mp"),
            P("dp", "mp"),
            P("mp", "dp"),
            P(),
            P("mp", None),
            P(),
            P(),
            P("dp", "mp"),
            P("dp"),
        ),
        out_specs=P("dp", None),
        check_vma=False,
    )
```

```python
import jax
import jax.numpy as jnp
from jax import lax
from jax.experimental import pallas as pl
from jax.experimental.pallas import tpu as pltpu
from jax.sharding import PartitionSpec as P

LANGS = 32
AXES = ("dp", "mp")
HIGH = lax.Precision.HIGHEST
F32 = jnp.float32


def flat(x, y, z, c):
    x, y, z = x % 4, y % 4, z % 8
    return (y * 4 + (z >> 1)) * 16 + x * 4 + (z & 1) * 2 + c


def perm_of(move):
    pairs = []
    for d in range(16):
        for m in range(16):
            place = (m >> 2, d >> 2, ((d & 3) << 1) | ((m >> 1) & 1), m & 1)
            there = move(*place)
            if there is not None:
                pairs.append((flat(*place), flat(*there)))
    return pairs


def send(v, move):
    return lax.ppermute(v, AXES, perm_of(move))


def first(v, *ready):
    return lax.optimization_barrier((v, *ready))


def ring_moves(axis):
    if axis == "x":
        return (lambda x, y, z, c: (x + 1, y, z, c)), (lambda x, y, z, c: (x - 1, y, z, c))
    return (lambda x, y, z, c: (x, y + 1, z, c)), (lambda x, y, z, c: (x, y - 1, z, c))


def ring_near(v, axis):
    plus, minus = ring_moves(axis)
    return send(v, plus), send(v, minus)


def ring_far(before, after, axis):
    plus, minus = ring_moves(axis)
    half = before.shape[0] // 2
    return send(before[:half], plus), send(after[half:], minus)


def weight_a(x, y, z, c):
    return (x, y, z + 4, c) if c == (z >> 1) & 1 else (x, y, z + 2, 1 - c)


def weight_b(x, y, z, c):
    return (x, y, z, c) if c == (z >> 1) & 1 else (x, y, z - 2, 1 - c)


def coords():
    d, m = lax.axis_index("dp"), lax.axis_index("mp")
    y, zhh, zhl = d // 4, (d // 2) % 2, d % 2
    x, zl, c = m // 4, (m // 2) % 2, m % 2
    return x, y, zhh, zhl, zl, c


def source_bit(zhh, zhl, c):
    same = (c + zhl + 1) % 2
    stays = (1 - same) * zhl
    return (zhh + 1 - stays) % 2


def token_copies(which, late, refs, xv, sem, x, zhh, zhl, zl, c):
    copies = []
    for s in range(2):
        low = (zl + s + (zl + zhl) % 2) % 2 if late else (zl + s) % 2
        for n, step in enumerate((0, 3, 1, 2)):
            col = pl.multiple_of((((x + step) % 4) * 2 + low) * 256, 256)
            for t in range(2):
                row = pl.multiple_of(((t + c) % 2) * 256, 256)
                if step == 2:
                    src = refs[s * 5 + 3 + which].at[pl.ds(t * 256, 256), :]
                else:
                    src = refs[s * 5 + n].at[pl.ds(which * 512 + t * 256, 256), :]
                dst = xv.at[pl.ds(row, 256), pl.ds(col, 256)]
                copies.append(pltpu.make_async_copy(src, dst, sem.at[(s * 4 + n) * 2 + t]))
    return copies


def gate_copies(ref, proj, wv, sem, bit, c):
    copies = []
    for n in range(8):
        src = proj.at[pl.ds(pl.multiple_of((n * 2 + c) * 256, 256), 256), :]
        copies.append(pltpu.make_async_copy(src, wv.at[pl.ds(n * 256, 256), pl.ds(896, 128)], sem.at[8 + n]))
    for r in range(2):
        h = bit if r == 0 else 1 - bit
        for n in range(4):
            row = pl.multiple_of((n * 2 + h) * 256, 256)
            copies.append(pltpu.make_async_copy(ref.at[n, r], wv.at[pl.ds(row, 256), pl.ds(0, 896)], sem.at[r * 4 + n]))
    return copies


def down_copies(ref, wv, sem, bit):
    copies = []
    for r in range(2):
        h = bit if r == 0 else 1 - bit
        for n in range(4):
            col = pl.multiple_of((n * 2 + h) * 256, 256)
            src = ref.at[n, r, pl.ds(0, 896), :]
            copies.append(pltpu.make_async_copy(src, wv.at[:, pl.ds(col, 256)], sem.at[r * 4 + n]))
    return copies


def gate_kernel(late, *refs):
    blocks, (weights, proj, _, keep, other, xv, wv, xsem, wsem) = refs[:10], refs[10:]
    x, y, zhh, zhl, zl, c = coords()
    copies = gate_copies(weights, proj, wv, wsem, source_bit(zhh, zhl, c), c)
    copies = copies + token_copies(0, late, blocks, xv, xsem, x, zhh, zhl, zl, c)
    for copy in copies:
        copy.start()
    for copy in copies:
        copy.wait()

    @pl.loop(0, 2)
    def _(i):
        rows = xv[pl.ds(pl.multiple_of(i * 256, 256), 256), :]
        product = jnp.dot(rows, wv[...], preferred_element_type=F32)
        for part, target in enumerate((keep, other)):
            @pl.when(i == part)
            def _():
                target[...] = product.astype(target.dtype)


def hidden_kernel(*refs):
    early, late, (weights, _, keep, other, xv, wv, xsem0, xsem1, wsem) = refs[:10], refs[10:20], refs[20:]
    x, y, zhh, zhl, zl, c = coords()
    first = down_copies(weights, wv, wsem, source_bit(zhh, zhl, c))
    first = first + token_copies(1, False, early, xv.at[pl.ds(0, 512), :], xsem0, x, zhh, zhl, zl, c)
    second = token_copies(1, True, late, xv.at[pl.ds(512, 512), :], xsem1, x, zhh, zhl, zl, c)
    for copy in first + second:
        copy.start()

    @pl.loop(0, 4)
    def _(i):
        for at, copies in ((0, first), (2, second)):
            @pl.when(i == at)
            def _():
                for copy in copies:
                    copy.wait()

        rows = xv[pl.ds(pl.multiple_of(i * 256, 256), 256), :]
        product = lax.dot_general(rows, wv[...], (((1,), (1,)), ((), ())), preferred_element_type=F32)
        place = pl.ds(pl.multiple_of((i // 2) * 256, 256), 256)
        for part, target in enumerate((keep, other)):
            @pl.when(i % 2 == part)
            def _():
                target[place, :] = product.astype(target.dtype)


def call(kernel, args, shape, scratch, flops):
    return pl.pallas_call(
        kernel,
        out_shape=[jax.ShapeDtypeStruct(shape, F32), jax.ShapeDtypeStruct(shape, jnp.bfloat16)],
        in_specs=[pl.BlockSpec(memory_space=pltpu.MemorySpace.HBM)] * len(args),
        out_specs=[pl.BlockSpec(memory_space=pltpu.VMEM)] * 2,
        scratch_shapes=scratch,
        compiler_params=pltpu.CompilerParams(vmem_limit_bytes=60 << 20),
        cost_estimate=pl.CostEstimate(flops=flops, bytes_accessed=8 << 20, transcendentals=0),
    )(*args)


def gate_matmul(late, blocks, weights, proj, after):
    scratch = [
        pltpu.VMEM((512, 2048), jnp.bfloat16),
        pltpu.VMEM((2048, 1024), jnp.bfloat16),
        pltpu.SemaphoreType.DMA((16,)),
        pltpu.SemaphoreType.DMA((16,)),
    ]
    kernel = lambda *refs: gate_kernel(late, *refs)
    return call(kernel, [*blocks, weights, proj, after], (256, 1024), scratch, 2 * 512 * 2048 * 1024)


def hidden_matmul(early, late, weights, after):
    scratch = [
        pltpu.VMEM((1024, 2048), jnp.bfloat16),
        pltpu.VMEM((896, 2048), jnp.bfloat16),
        pltpu.SemaphoreType.DMA((16,)),
        pltpu.SemaphoreType.DMA((16,)),
        pltpu.SemaphoreType.DMA((8,)),
    ]
    return call(hidden_kernel, [*early, *late, weights, after], (512, 896), scratch, 2 * 1024 * 2048 * 896)


def everyone(v, axis):
    return lax.all_to_all(jnp.broadcast_to(v[None], (16,) + v.shape), axis, 0, 0, tiled=True)


def shards(inputs, out_grads, gate_weight, down_weight, in_proj, out_proj, in_precond, out_precond, queries, languages):
    x, y, zhh, zhl, zl, c = coords()
    swap = lambda x, y, z, c: (x, y, z, 1 - c)
    rings = [[y * 4 + h for y in range(4)] for h in range(4)]

    hold = lax.optimization_barrier
    in_proj = jnp.pad(in_proj, ((0, 0), (0, 64)))
    with jax.named_scope("language_sums"):
        onehot = (languages[None, :] == jnp.arange(LANGS, dtype=jnp.int32)[:, None]).astype(jnp.bfloat16)
        mine = jnp.dot(onehot, queries, preferred_element_type=F32)
        high = lax.reduce_precision(mine, 8, 7)
        halves = [high.astype(jnp.bfloat16), (mine - high).astype(jnp.bfloat16)]
        down_weight = jnp.concatenate([down_weight, *halves], axis=0)
    inward = lambda x, y, z, c: (x, y, z ^ 3, c) if z % 4 in (1, 2) else None
    outward = lambda x, y, z, c: (x, y, z ^ 1, c) if z % 4 in (1, 2) else None
    with jax.named_scope("first_moves"):
        ga = send(gate_weight, weight_a)
        gb = send(gate_weight, weight_b)
        both = jnp.concatenate([inputs[0], out_grads[0]], axis=0)
        near = send(both, lambda x, y, z, c: (x, y, z ^ 1, c))
        inner_a = send(both, inward)
        own1, own2 = ring_near(both, "x")
        gates = lax.all_gather(jnp.stack([ga, gb]), "dp", axis_index_groups=rings)
        out_mine = jnp.where(c == zhl, out_proj, send(out_proj, swap))
        near, inner_a, own1, own2, down_weight, out_mine, in_proj, ga = hold(
            (near, inner_a, own1, own2, down_weight, out_mine, in_proj, ga)
        )
    with jax.named_scope("second_moves"):
        da = send(down_weight, weight_a)
        db = send(down_weight, weight_b)
        inner_b = send(near, inward)
        outer_a = send(inner_a, outward)
        near1, near2 = ring_near(near, "x")
        inner_b, outer_a, da, db, near1, near2 = hold((inner_b, outer_a, da, db, near1, near2))
    with jax.named_scope("third_moves"):
        downs = lax.all_gather(jnp.stack([da, db]), "dp", axis_index_groups=rings)
        far_a = jnp.where(zl == zhl, outer_a, inner_a)
        outer_b = send(inner_b, outward)
        fa1, fa2 = ring_near(far_a, "x")
        near3, near4 = ring_far(near1, near2, "x")
        own3, own4 = ring_far(own1, own2, "x")
        outer_b, fa1, fa2, near3, near4, own3, own4 = hold((outer_b, fa1, fa2, near3, near4, own3, own4))
    early = [both, own1, own2, own3, own4, near, near1, near2, near3, near4]
    with jax.named_scope("fourth_moves"):
        far_b = jnp.where(zl == zhl, outer_b, inner_b)
        fb1, fb2 = ring_near(far_b, "x")
        fa3, fa4 = ring_far(fa1, fa2, "x")
        gate0 = gate_matmul(False, early, gates, in_proj, fa1)
        fb1, fb2, fa3, fa4, *gate0 = hold((fb1, fb2, fa3, fa4, *gate0))
    with jax.named_scope("fifth_moves"):
        fb3, fb4 = ring_far(fb1, fb2, "x")
        late = [far_a, fa1, fa2, fa3, fa4, far_b, fb1, fb2, fb3, fb4]
        first = send(gate0[1], swap)
        gate1 = gate_matmul(True, late, gates, in_proj, first)
    with jax.named_scope("hidden"):
        hidden, other = hidden_matmul(early, late, downs, gate1[1])
        gate_both = [gate0[0] + first.astype(F32), gate1[0] + send(gate1[1], swap).astype(F32)]
        hidden = hidden + send(other, swap).astype(F32)
        downs, other = hold((downs, other))
        sums = jnp.sum(downs[:, :, 896:].astype(F32).reshape(16, LANGS, 256), axis=0)
        sums = sums + send(sums, swap)

    def finish(gate, hidden_grad):
        up_grad = (hidden_grad * jax.nn.silu(gate[:, :896])).astype(jnp.bfloat16)
        out_part = jnp.dot(up_grad, out_mine, preferred_element_type=F32)
        return lax.dot_general(gate[:, 896:960], out_part, (((0,), (0,)), ((), ())), precision=HIGH)

    with jax.named_scope("second_half"):
        outer1 = finish(gate_both[1], hidden[256:])
    with jax.named_scope("first_half"):
        outer0 = finish(gate_both[0], hidden[:256])

    with jax.named_scope("finish"):
        moved = jnp.concatenate([jnp.pad(outer1, ((0, 0), (0, 192))), sums], axis=0)
        moved = send(moved, lambda x, y, z, c: (x, y, z ^ 2, c))
        outers = outer0 + moved[:64, :64]
        by_language = jnp.where(c == zhl, sums, moved[64:])
        part = jnp.dot(jnp.dot(in_precond, outers, precision=HIGH), out_precond, precision=HIGH) / 512
        bands = lax.all_to_all(part.reshape(16, 256), "mp", 0, 0, tiled=True)
        projected = lax.reduce_precision(jnp.sum(bands, axis=0), 8, 7)
        scores = jnp.sum(projected[None, :] * by_language, axis=1)
        scores = jnp.sum(everyone(scores, "mp").reshape(16, LANGS), axis=0)
    return (scores / 64).reshape(1, LANGS)


def solution(mesh):
    return jax.shard_map(
        shards,
        mesh=mesh,
        in_specs=(
            P("dp", None, "mp"),
            P("dp", None, "mp"),
            P("dp", "mp"),
            P("mp", "dp"),
            P(),
            P("mp", None),
            P(),
            P(),
            P("dp", "mp"),
            P("dp"),
        ),
        out_specs=P("dp", None),
        check_vma=False,
    )
```

```python
import jax
import jax.numpy as jnp
from jax import lax
from jax.experimental import pallas as pl
from jax.experimental.pallas import tpu as pltpu
from jax.sharding import PartitionSpec as P

LANGS = 32
AXES = ("dp", "mp")
HIGH = lax.Precision.HIGHEST
F32 = jnp.float32


def flat(x, y, z, c):
    x, y, z = x % 4, y % 4, z % 8
    return (y * 4 + (z >> 1)) * 16 + x * 4 + (z & 1) * 2 + c


def perm_of(move):
    pairs = []
    for d in range(16):
        for m in range(16):
            place = (m >> 2, d >> 2, ((d & 3) << 1) | ((m >> 1) & 1), m & 1)
            there = move(*place)
            if there is not None:
                pairs.append((flat(*place), flat(*there)))
    return pairs


def send(v, move):
    return lax.ppermute(v, AXES, perm_of(move))


def first(v, *ready):
    return lax.optimization_barrier((v, *ready))


def ring_moves(axis):
    if axis == "x":
        return (lambda x, y, z, c: (x + 1, y, z, c)), (lambda x, y, z, c: (x - 1, y, z, c))
    return (lambda x, y, z, c: (x, y + 1, z, c)), (lambda x, y, z, c: (x, y - 1, z, c))


def ring_near(v, axis):
    plus, minus = ring_moves(axis)
    return send(v, plus), send(v, minus)


def ring_far(before, after, axis):
    plus, minus = ring_moves(axis)
    half = before.shape[0] // 2
    return send(before[:half], plus), send(after[half:], minus)


def weight_a(x, y, z, c):
    return (x, y, z + 4, c) if c == (z >> 1) & 1 else (x, y, z + 2, 1 - c)


def weight_b(x, y, z, c):
    return (x, y, z, c) if c == (z >> 1) & 1 else (x, y, z - 2, 1 - c)


def coords():
    d, m = lax.axis_index("dp"), lax.axis_index("mp")
    y, zhh, zhl = d // 4, (d // 2) % 2, d % 2
    x, zl, c = m // 4, (m // 2) % 2, m % 2
    return x, y, zhh, zhl, zl, c


def source_bit(zhh, zhl, c):
    same = (c + zhl + 1) % 2
    stays = (1 - same) * zhl
    return (zhh + 1 - stays) % 2


def token_copies(which, late, refs, xv, sem, x, zhh, zhl, zl, c):
    copies = []
    for s in range(2):
        low = (zl + s + (zl + zhl) % 2) % 2 if late else (zl + s) % 2
        for n, step in enumerate((0, 3, 1, 2)):
            col = pl.multiple_of((((x + step) % 4) * 2 + low) * 256, 256)
            for t in range(2):
                row = pl.multiple_of(((t + c) % 2) * 256, 256)
                if step == 2:
                    src = refs[s * 5 + 3 + which].at[pl.ds(t * 256, 256), :]
                else:
                    src = refs[s * 5 + n].at[pl.ds(which * 512 + t * 256, 256), :]
                dst = xv.at[pl.ds(row, 256), pl.ds(col, 256)]
                copies.append(pltpu.make_async_copy(src, dst, sem.at[(s * 4 + n) * 2 + t]))
    return copies


def gate_copies(ref, proj, wv, sem, bit, c):
    copies = []
    for n in range(8):
        src = proj.at[pl.ds(pl.multiple_of((n * 2 + c) * 256, 256), 256), :]
        copies.append(pltpu.make_async_copy(src, wv.at[pl.ds(n * 256, 256), pl.ds(896, 128)], sem.at[8 + n]))
    for r in range(2):
        h = bit if r == 0 else 1 - bit
        for n in range(4):
            row = pl.multiple_of((n * 2 + h) * 256, 256)
            copies.append(pltpu.make_async_copy(ref.at[n, r], wv.at[pl.ds(row, 256), pl.ds(0, 896)], sem.at[r * 4 + n]))
    return copies


def down_copies(ref, wv, sem, bit):
    copies = []
    for r in range(2):
        h = bit if r == 0 else 1 - bit
        for n in range(4):
            col = pl.multiple_of((n * 2 + h) * 256, 256)
            src = ref.at[n, r, pl.ds(0, 896), :]
            copies.append(pltpu.make_async_copy(src, wv.at[:, pl.ds(col, 256)], sem.at[r * 4 + n]))
    return copies


def gate_kernel(late, *refs):
    blocks, (weights, proj, _, keep, other, xv, wv, xsem, wsem) = refs[:10], refs[10:]
    x, y, zhh, zhl, zl, c = coords()
    copies = gate_copies(weights, proj, wv, wsem, source_bit(zhh, zhl, c), c)
    copies = copies + token_copies(0, late, blocks, xv, xsem, x, zhh, zhl, zl, c)
    for copy in copies:
        copy.start()
    for copy in copies:
        copy.wait()

    @pl.loop(0, 2)
    def _(i):
        rows = xv[pl.ds(pl.multiple_of(i * 256, 256), 256), :]
        product = jnp.dot(rows, wv[...], preferred_element_type=F32)
        for part, target in enumerate((keep, other)):
            @pl.when(i == part)
            def _():
                target[...] = product.astype(target.dtype)


def hidden_kernel(*refs):
    early, late, (weights, _, keep, other, xv, wv, xsem0, xsem1, wsem) = refs[:10], refs[10:20], refs[20:]
    x, y, zhh, zhl, zl, c = coords()
    first = down_copies(weights, wv, wsem, source_bit(zhh, zhl, c))
    first = first + token_copies(1, False, early, xv.at[pl.ds(0, 512), :], xsem0, x, zhh, zhl, zl, c)
    second = token_copies(1, True, late, xv.at[pl.ds(512, 512), :], xsem1, x, zhh, zhl, zl, c)
    for copy in first + second:
        copy.start()

    @pl.loop(0, 4)
    def _(i):
        for at, copies in ((0, first), (2, second)):
            @pl.when(i == at)
            def _():
                for copy in copies:
                    copy.wait()

        rows = xv[pl.ds(pl.multiple_of(i * 256, 256), 256), :]
        product = lax.dot_general(rows, wv[...], (((1,), (1,)), ((), ())), preferred_element_type=F32)
        place = pl.ds(pl.multiple_of((i // 2) * 256, 256), 256)
        for part, target in enumerate((keep, other)):
            @pl.when(i % 2 == part)
            def _():
                target[place, :] = product.astype(target.dtype)


def call(kernel, args, shape, scratch, flops):
    return pl.pallas_call(
        kernel,
        out_shape=[jax.ShapeDtypeStruct(shape, F32)] * 2,
        in_specs=[pl.BlockSpec(memory_space=pltpu.MemorySpace.HBM)] * len(args),
        out_specs=[pl.BlockSpec(memory_space=pltpu.VMEM)] * 2,
        scratch_shapes=scratch,
        compiler_params=pltpu.CompilerParams(vmem_limit_bytes=60 << 20),
        cost_estimate=pl.CostEstimate(flops=flops, bytes_accessed=8 << 20, transcendentals=0),
    )(*args)


def gate_matmul(late, blocks, weights, proj, after):
    scratch = [
        pltpu.VMEM((512, 2048), jnp.bfloat16),
        pltpu.VMEM((2048, 1024), jnp.bfloat16),
        pltpu.SemaphoreType.DMA((16,)),
        pltpu.SemaphoreType.DMA((16,)),
    ]
    kernel = lambda *refs: gate_kernel(late, *refs)
    return call(kernel, [*blocks, weights, proj, after], (256, 1024), scratch, 2 * 512 * 2048 * 1024)


def hidden_matmul(early, late, weights, after):
    scratch = [
        pltpu.VMEM((1024, 2048), jnp.bfloat16),
        pltpu.VMEM((896, 2048), jnp.bfloat16),
        pltpu.SemaphoreType.DMA((16,)),
        pltpu.SemaphoreType.DMA((16,)),
        pltpu.SemaphoreType.DMA((8,)),
    ]
    return call(hidden_kernel, [*early, *late, weights, after], (512, 896), scratch, 2 * 1024 * 2048 * 896)


def everyone(v, axis):
    return lax.all_to_all(jnp.broadcast_to(v[None], (16,) + v.shape), axis, 0, 0, tiled=True)


def shards(inputs, out_grads, gate_weight, down_weight, in_proj, out_proj, in_precond, out_precond, queries, languages):
    x, y, zhh, zhl, zl, c = coords()
    swap = lambda x, y, z, c: (x, y, z, 1 - c)
    rings = [[y * 4 + h for y in range(4)] for h in range(4)]

    hold = lax.optimization_barrier
    in_proj = jnp.pad(in_proj, ((0, 0), (0, 64)))
    with jax.named_scope("language_sums"):
        onehot = (languages[None, :] == jnp.arange(LANGS, dtype=jnp.int32)[:, None]).astype(jnp.bfloat16)
        mine = jnp.dot(onehot, queries, preferred_element_type=F32)
        high = lax.reduce_precision(mine, 8, 7)
        halves = [high.astype(jnp.bfloat16), (mine - high).astype(jnp.bfloat16)]
        down_weight = jnp.concatenate([down_weight, *halves], axis=0)
    inward = lambda x, y, z, c: (x, y, z ^ 3, c) if z % 4 in (1, 2) else None
    outward = lambda x, y, z, c: (x, y, z ^ 1, c) if z % 4 in (1, 2) else None
    with jax.named_scope("first_moves"):
        ga = send(gate_weight, weight_a)
        gb = send(gate_weight, weight_b)
        both = jnp.concatenate([inputs[0], out_grads[0]], axis=0)
        near = send(both, lambda x, y, z, c: (x, y, z ^ 1, c))
        inner_a = send(both, inward)
        own1, own2 = ring_near(both, "x")
        out_mine = jnp.where(c == zhl, out_proj, send(out_proj, swap))
        ga, gb, own1, own2, out_mine, in_proj, down_weight = hold((ga, gb, own1, own2, out_mine, in_proj, down_weight))
        gates = lax.all_gather(jnp.stack([ga, gb]), "dp", axis_index_groups=rings)
        near, inner_a, own1, own2, down_weight, out_mine, in_proj, ga = hold(
            (near, inner_a, own1, own2, down_weight, out_mine, in_proj, ga)
        )
    with jax.named_scope("second_moves"):
        da = send(down_weight, weight_a)
        db = send(down_weight, weight_b)
        inner_b = send(near, inward)
        outer_a = send(inner_a, outward)
        near1, near2 = ring_near(near, "x")
        inner_b, outer_a, da, db, near1, near2 = hold((inner_b, outer_a, da, db, near1, near2))
    with jax.named_scope("third_moves"):
        downs = lax.all_gather(jnp.stack([da, db]), "dp", axis_index_groups=rings)
        far_a = jnp.where(zl == zhl, outer_a, inner_a)
        outer_b = send(inner_b, outward)
        fa1, fa2 = ring_near(far_a, "x")
        near3, near4 = ring_far(near1, near2, "x")
        own3, own4 = ring_far(own1, own2, "x")
        outer_b, fa1, fa2, near3, near4, own3, own4 = hold((outer_b, fa1, fa2, near3, near4, own3, own4))
    early = [both, own1, own2, own3, own4, near, near1, near2, near3, near4]
    with jax.named_scope("fourth_moves"):
        far_b = jnp.where(zl == zhl, outer_b, inner_b)
        fb1, fb2 = ring_near(far_b, "x")
        fa3, fa4 = ring_far(fa1, fa2, "x")
        gate0 = gate_matmul(False, early, gates, in_proj, fa1)
        fb1, fb2, fa3, fa4, *gate0 = hold((fb1, fb2, fa3, fa4, *gate0))
    with jax.named_scope("fifth_moves"):
        fb3, fb4 = ring_far(fb1, fb2, "x")
        late = [far_a, fa1, fa2, fa3, fa4, far_b, fb1, fb2, fb3, fb4]
        first = send(gate0[1], swap)
        gate1 = gate_matmul(True, late, gates, in_proj, first)
    with jax.named_scope("hidden"):
        hidden, other = hidden_matmul(early, late, downs, gate1[1])
        gate_both = [gate0[0] + first, gate1[0] + send(gate1[1], swap)]
        hidden = hidden + send(other, swap)
        downs, other = hold((downs, other))
        sums = jnp.sum(downs[:, :, 896:].astype(F32).reshape(16, LANGS, 256), axis=0)
        sums = sums + send(sums, swap)

    def finish(gate, hidden_grad):
        up_grad = (hidden_grad * jax.nn.silu(gate[:, :896])).astype(jnp.bfloat16)
        out_part = jnp.dot(up_grad, out_mine, preferred_element_type=F32)
        return lax.dot_general(gate[:, 896:960], out_part, (((0,), (0,)), ((), ())), precision=HIGH)

    with jax.named_scope("second_half"):
        outer1 = finish(gate_both[1], hidden[256:])
    with jax.named_scope("first_half"):
        outer0 = finish(gate_both[0], hidden[:256])

    with jax.named_scope("finish"):
        moved = jnp.concatenate([jnp.pad(outer1, ((0, 0), (0, 192))), sums], axis=0)
        moved = send(moved, lambda x, y, z, c: (x, y, z ^ 2, c))
        outers = outer0 + moved[:64, :64]
        by_language = jnp.where(c == zhl, sums, moved[64:])
        part = jnp.dot(jnp.dot(in_precond, outers, precision=HIGH), out_precond, precision=HIGH) / 512
        bands = lax.all_to_all(part.reshape(16, 256), "mp", 0, 0, tiled=True)
        projected = lax.reduce_precision(jnp.sum(bands, axis=0), 8, 7)
        scores = jnp.sum(projected[None, :] * by_language, axis=1)
        scores = jnp.sum(everyone(scores, "mp").reshape(16, LANGS), axis=0)
    return (scores / 64).reshape(1, LANGS)


def solution(mesh):
    return jax.shard_map(
        shards,
        mesh=mesh,
        in_specs=(
            P("dp", None, "mp"),
            P("dp", None, "mp"),
            P("dp", "mp"),
            P("mp", "dp"),
            P(),
            P("mp", None),
            P(),
            P(),
            P("dp", "mp"),
            P("dp"),
        ),
        out_specs=P("dp", None),
        check_vma=False,
    )
```

```python
import jax
import jax.numpy as jnp
from jax import lax
from jax.experimental import pallas as pl
from jax.experimental.pallas import tpu as pltpu
from jax.sharding import PartitionSpec as P

LANGS = 32
AXES = ("dp", "mp")
HIGH = lax.Precision.HIGHEST
F32 = jnp.float32


def flat(x, y, z, c):
    x, y, z = x % 4, y % 4, z % 8
    return (y * 4 + (z >> 1)) * 16 + x * 4 + (z & 1) * 2 + c


def perm_of(move):
    pairs = []
    for d in range(16):
        for m in range(16):
            place = (m >> 2, d >> 2, ((d & 3) << 1) | ((m >> 1) & 1), m & 1)
            there = move(*place)
            if there is not None:
                pairs.append((flat(*place), flat(*there)))
    return pairs


def send(v, move):
    return lax.ppermute(v, AXES, perm_of(move))


def first(v, *ready):
    return lax.optimization_barrier((v, *ready))


def ring_moves(axis):
    if axis == "x":
        return (lambda x, y, z, c: (x + 1, y, z, c)), (lambda x, y, z, c: (x - 1, y, z, c))
    return (lambda x, y, z, c: (x, y + 1, z, c)), (lambda x, y, z, c: (x, y - 1, z, c))


def ring_near(v, axis):
    plus, minus = ring_moves(axis)
    return send(v, plus), send(v, minus)


def ring_far(before, after, axis):
    plus, minus = ring_moves(axis)
    half = before.shape[0] // 2
    return send(before[:half], plus), send(after[half:], minus)


def weight_a(x, y, z, c):
    return (x, y, z + 4, c) if c == (z >> 1) & 1 else (x, y, z + 2, 1 - c)


def weight_b(x, y, z, c):
    return (x, y, z, c) if c == (z >> 1) & 1 else (x, y, z - 2, 1 - c)


def coords():
    d, m = lax.axis_index("dp"), lax.axis_index("mp")
    y, zhh, zhl = d // 4, (d // 2) % 2, d % 2
    x, zl, c = m // 4, (m // 2) % 2, m % 2
    return x, y, zhh, zhl, zl, c


def source_bit(zhh, zhl, c):
    same = (c + zhl + 1) % 2
    stays = (1 - same) * zhl
    return (zhh + 1 - stays) % 2


def token_copies(which, late, refs, xv, sem, x, zhh, zhl, zl, c):
    copies = []
    for s in range(2):
        low = (zl + s + (zl + zhl) % 2) % 2 if late else (zl + s) % 2
        for n, step in enumerate((0, 3, 1, 2)):
            col = pl.multiple_of((((x + step) % 4) * 2 + low) * 256, 256)
            for t in range(2):
                row = pl.multiple_of(((t + c) % 2) * 256, 256)
                if step == 2:
                    src = refs[s * 5 + 3 + which].at[pl.ds(t * 256, 256), :]
                else:
                    src = refs[s * 5 + n].at[pl.ds(which * 512 + t * 256, 256), :]
                dst = xv.at[pl.ds(row, 256), pl.ds(col, 256)]
                copies.append(pltpu.make_async_copy(src, dst, sem.at[(s * 4 + n) * 2 + t]))
    return copies


def gate_copies(ref, proj, wv, sem, bit, c):
    copies = []
    for n in range(8):
        src = proj.at[pl.ds(pl.multiple_of((n * 2 + c) * 256, 256), 256), :]
        copies.append(pltpu.make_async_copy(src, wv.at[pl.ds(n * 256, 256), pl.ds(896, 128)], sem.at[8 + n]))
    for r in range(2):
        h = bit if r == 0 else 1 - bit
        for n in range(4):
            row = pl.multiple_of((n * 2 + h) * 256, 256)
            copies.append(pltpu.make_async_copy(ref.at[n, r], wv.at[pl.ds(row, 256), pl.ds(0, 896)], sem.at[r * 4 + n]))
    return copies


def down_copies(ref, wv, sem, bit):
    copies = []
    for r in range(2):
        h = bit if r == 0 else 1 - bit
        for n in range(4):
            col = pl.multiple_of((n * 2 + h) * 256, 256)
            src = ref.at[n, r, pl.ds(0, 896), :]
            copies.append(pltpu.make_async_copy(src, wv.at[:, pl.ds(col, 256)], sem.at[r * 4 + n]))
    return copies


def gate_kernel(late, *refs):
    blocks, (weights, proj, _, keep, other, xv, wv, xsem, wsem) = refs[:10], refs[10:]
    x, y, zhh, zhl, zl, c = coords()
    copies = gate_copies(weights, proj, wv, wsem, source_bit(zhh, zhl, c), c)
    copies = copies + token_copies(0, late, blocks, xv, xsem, x, zhh, zhl, zl, c)
    for copy in copies:
        copy.start()
    for copy in copies:
        copy.wait()

    @pl.loop(0, 2)
    def _(i):
        rows = xv[pl.ds(pl.multiple_of(i * 256, 256), 256), :]
        product = jnp.dot(rows, wv[...], preferred_element_type=F32)
        for part, target in enumerate((keep, other)):
            @pl.when(i == part)
            def _():
                target[...] = product.astype(target.dtype)


def hidden_kernel(*refs):
    early, late, (weights, _, keep, other, xv, wv, xsem0, xsem1, wsem) = refs[:10], refs[10:20], refs[20:]
    x, y, zhh, zhl, zl, c = coords()
    first = down_copies(weights, wv, wsem, source_bit(zhh, zhl, c))
    first = first + token_copies(1, False, early, xv.at[pl.ds(0, 512), :], xsem0, x, zhh, zhl, zl, c)
    second = token_copies(1, True, late, xv.at[pl.ds(512, 512), :], xsem1, x, zhh, zhl, zl, c)
    for copy in first + second:
        copy.start()

    @pl.loop(0, 4)
    def _(i):
        for at, copies in ((0, first), (2, second)):
            @pl.when(i == at)
            def _():
                for copy in copies:
                    copy.wait()

        rows = xv[pl.ds(pl.multiple_of(i * 256, 256), 256), :]
        product = lax.dot_general(rows, wv[...], (((1,), (1,)), ((), ())), preferred_element_type=F32)
        place = pl.ds(pl.multiple_of((i // 2) * 256, 256), 256)
        for part, target in enumerate((keep, other)):
            @pl.when(i % 2 == part)
            def _():
                target[place, :] = product.astype(target.dtype)


def call(kernel, args, shape, scratch, flops):
    return pl.pallas_call(
        kernel,
        out_shape=[jax.ShapeDtypeStruct(shape, F32)] * 2,
        in_specs=[pl.BlockSpec(memory_space=pltpu.MemorySpace.HBM)] * len(args),
        out_specs=[pl.BlockSpec(memory_space=pltpu.VMEM)] * 2,
        scratch_shapes=scratch,
        compiler_params=pltpu.CompilerParams(vmem_limit_bytes=60 << 20),
        cost_estimate=pl.CostEstimate(flops=flops, bytes_accessed=8 << 20, transcendentals=0),
    )(*args)


def gate_matmul(late, blocks, weights, proj, after):
    scratch = [
        pltpu.VMEM((512, 2048), jnp.bfloat16),
        pltpu.VMEM((2048, 1024), jnp.bfloat16),
        pltpu.SemaphoreType.DMA((16,)),
        pltpu.SemaphoreType.DMA((16,)),
    ]
    kernel = lambda *refs: gate_kernel(late, *refs)
    return call(kernel, [*blocks, weights, proj, after], (256, 1024), scratch, 2 * 512 * 2048 * 1024)


def hidden_matmul(early, late, weights, after):
    scratch = [
        pltpu.VMEM((1024, 2048), jnp.bfloat16),
        pltpu.VMEM((896, 2048), jnp.bfloat16),
        pltpu.SemaphoreType.DMA((16,)),
        pltpu.SemaphoreType.DMA((16,)),
        pltpu.SemaphoreType.DMA((8,)),
    ]
    return call(hidden_kernel, [*early, *late, weights, after], (512, 896), scratch, 2 * 1024 * 2048 * 896)


def everyone(v, axis):
    return lax.all_to_all(jnp.broadcast_to(v[None], (16,) + v.shape), axis, 0, 0, tiled=True)


def shards(inputs, out_grads, gate_weight, down_weight, in_proj, out_proj, in_precond, out_precond, queries, languages):
    x, y, zhh, zhl, zl, c = coords()
    swap = lambda x, y, z, c: (x, y, z, 1 - c)
    rings = [[y * 4 + h for y in range(4)] for h in range(4)]

    hold = lax.optimization_barrier
    in_proj = jnp.pad(in_proj, ((0, 0), (0, 64)))
    with jax.named_scope("language_sums"):
        onehot = (languages[None, :] == jnp.arange(LANGS, dtype=jnp.int32)[:, None]).astype(jnp.bfloat16)
        mine = jnp.dot(onehot, queries, preferred_element_type=F32)
        high = lax.reduce_precision(mine, 8, 7)
        halves = [high.astype(jnp.bfloat16), (mine - high).astype(jnp.bfloat16)]
        down_weight = jnp.concatenate([down_weight, *halves], axis=0)
    inward = lambda x, y, z, c: (x, y, z ^ 3, c) if z % 4 in (1, 2) else None
    outward = lambda x, y, z, c: (x, y, z ^ 1, c) if z % 4 in (1, 2) else None
    with jax.named_scope("first_moves"):
        ga = send(gate_weight, weight_a)
        gb = send(gate_weight, weight_b)
        both = jnp.concatenate([inputs[0], out_grads[0]], axis=0)
        near = send(both, lambda x, y, z, c: (x, y, z ^ 1, c))
        inner_a = send(both, inward)
        own1, own2 = ring_near(both, "x")
        gates = lax.all_gather(jnp.stack([ga, gb]), "dp", axis_index_groups=rings)
        out_mine = jnp.where(c == zhl, out_proj, send(out_proj, swap))
        near, inner_a, own1, own2, down_weight, out_mine, in_proj, ga = hold(
            (near, inner_a, own1, own2, down_weight, out_mine, in_proj, ga)
        )
    with jax.named_scope("second_moves"):
        da = send(down_weight, weight_a)
        db = send(down_weight, weight_b)
        inner_b = send(near, inward)
        outer_a = send(inner_a, outward)
        near1, near2 = ring_near(near, "x")
        inner_b, outer_a, da, db, near1, near2 = hold((inner_b, outer_a, da, db, near1, near2))
    with jax.named_scope("third_moves"):
        downs = lax.all_gather(jnp.stack([da, db]), "dp", axis_index_groups=rings)
        far_a = jnp.where(zl == zhl, outer_a, inner_a)
        outer_b = send(inner_b, outward)
        fa1, fa2 = ring_near(far_a, "x")
        near3, near4 = ring_far(near1, near2, "x")
        own3, own4 = ring_far(own1, own2, "x")
        outer_b, fa1, fa2, near3, near4, own3, own4 = hold((outer_b, fa1, fa2, near3, near4, own3, own4))
    early = [both, own1, own2, own3, own4, near, near1, near2, near3, near4]
    with jax.named_scope("fourth_moves"):
        far_b = jnp.where(zl == zhl, outer_b, inner_b)
        fb1, fb2 = ring_near(far_b, "x")
        fa3, fa4 = ring_far(fa1, fa2, "x")
        gate0 = gate_matmul(False, early, gates, in_proj, fa1)
        fb1, fb2, fa3, fa4, *gate0 = hold((fb1, fb2, fa3, fa4, *gate0))
    with jax.named_scope("fifth_moves"):
        fb3, fb4 = ring_far(fb1, fb2, "x")
        late = [far_a, fa1, fa2, fa3, fa4, far_b, fb1, fb2, fb3, fb4]
        first = send(gate0[1], swap)
        gate1 = gate_matmul(True, late, gates, in_proj, first)
    with jax.named_scope("hidden"):
        hidden, other = hidden_matmul(early, late, downs, gate1[1])
        gate_both = [gate0[0] + first, gate1[0] + send(gate1[1], swap)]
        hidden = hidden + send(other, swap)
        downs, other = hold((downs, other))
        sums = jnp.sum(downs[:, :, 896:].astype(F32).reshape(16, LANGS, 256), axis=0)
        sums = sums + send(sums, swap)

    def finish(gate, hidden_grad):
        up_grad = (hidden_grad * jax.nn.silu(gate[:, :896])).astype(jnp.bfloat16)
        out_part = jnp.dot(up_grad, out_mine, preferred_element_type=F32)
        return lax.dot_general(gate[:, 896:960], out_part, (((0,), (0,)), ((), ())), precision=HIGH)

    with jax.named_scope("second_half"):
        outer1 = finish(gate_both[1], hidden[256:])
    with jax.named_scope("first_half"):
        outer0 = finish(gate_both[0], hidden[:256])

    with jax.named_scope("finish"):
        moved = jnp.concatenate([jnp.pad(outer1, ((0, 0), (0, 192))), sums], axis=0)
        moved = send(moved, lambda x, y, z, c: (x, y, z ^ 2, c))
        outers = outer0 + moved[:64, :64]
        by_language = jnp.where(c == zhl, sums, moved[64:])
        part = jnp.dot(jnp.dot(in_precond, outers, precision=HIGH), out_precond, precision=HIGH) / 512
        bands = lax.all_to_all(part.reshape(16, 256), "mp", 0, 0, tiled=True)
        projected = lax.reduce_precision(jnp.sum(bands, axis=0), 8, 7)
        scores = jnp.sum(projected[None, :] * by_language, axis=1)
        scores = jnp.sum(everyone(scores, "mp").reshape(16, LANGS), axis=0)
    return (scores / 64).reshape(1, LANGS)


def solution(mesh):
    return jax.shard_map(
        shards,
        mesh=mesh,
        in_specs=(
            P("dp", None, "mp"),
            P("dp", None, "mp"),
            P("dp", "mp"),
            P("mp", "dp"),
            P(),
            P("mp", None),
            P(),
            P(),
            P("dp", "mp"),
            P("dp"),
        ),
        out_specs=P("dp", None),
        check_vma=False,
    )
```
